32 devices in a mesh: row: 4 (over z), col: 8 (over y, x, core).
Axes of the slice: x: 2, y: 2, z: 4, core: 2. Of those that a mesh axis runs over, the one named last changes fastest.
Arguments:
- pair_state: bfloat16 [384, 384, 128], P('row', 'col'), may hold values from -40 to 40
- seq_state: bfloat16 [384, 1024], P('row', 'col'), may hold values from -40 to 40
- residue_index: int32 [384], replicated, may hold values from 0 to 1535, as said below
- residue_mask: int32 [384], replicated, may hold values from 0 to 1, as said below
- position_table: bfloat16 [66, 128], replicated, may hold values from -4 to 4
- attention_gain: float32 [2, 1024], replicated, may hold values from 0.1 to 1.9
- bias_norm_gain: float32 [2, 128], replicated, may hold values from 0.1 to 1.9
- query_weight: bfloat16 [2, 1024, 1024], P(None, None, 'col'), may hold values from -16 to 16
- key_weight: bfloat16 [2, 1024, 1024], P(None, None, 'col'), may hold values from -1 to 1
- value_weight: bfloat16 [2, 1024, 1024], P(None, None, 'col'), may hold values from -0.1875 to 0.1875
- gate_weight: bfloat16 [2, 1024, 1024], P(None, None, 'col'), may hold values from -0.1875 to 0.1875
- out_weight: bfloat16 [2, 1024, 1024], P(None, None, 'col'), may hold values from -0.75 to 0.75
- bias_weight: bfloat16 [2, 128, 32], replicated, may hold values from -1.5 to 1.5
- outer_gain: float32 [2, 1024], replicated, may hold values from 0.1 to 1.9
- outer_weight: bfloat16 [2, 1024, 128], replicated, may hold values from -0.1875 to 0.1875
- outer_out_weight: bfloat16 [2, 128, 128], replicated, may hold values from -0.5 to 0.5
- transition_gain: float32 [2, 128], replicated, may hold values from 0.1 to 1.9
- up_weight: bfloat16 [2, 128, 512], replicated, may hold values from -0.5 to 0.5
- down_weight: bfloat16 [2, 512, 128], replicated, may hold values from -0.25 to 0.25
- distance_weight: bfloat16 [128, 64], replicated, may hold values from -0.5 to 0.5
Outputs:
- distogram: bfloat16 [384, 384, 64], P('row', 'col')
- seq_out: bfloat16 [384, 1024], P('row', 'col')
The draws below stay inside these ranges and needn't reach their ends.
Inputs may be any that keep to these rules, and one draw needn't show every extreme that they name: `residue_index`: strictly increasing; the first entry is 0 and the last is 1535. `residue_mask`: 1 on a prefix of 192 to 383 residues and 0 after it.
All inputs are finite; a program needn't handle non-finite values.
Results may differ from the reference program's by a relative error of at most 0.028.
Values may be sent and summed in bfloat16 or wider, within the bound.
A program may use at most 64 MiB of HBM per device.

```python
import jax
import jax.numpy as jnp
from jax import lax

CS = 1024
HEAD_DIM = 32
CZ = 128
BINS = 64
RELPOS_MAX = 32
LAYERS = 2
HEADS = 32
INNER = 64
FFZ = 512
RELPOS_BINS = 66
LENGTH = 384
N_ROW = 4


def draw_pair_state(key, part):
    base_key = jax.random.fold_in(jax.random.fold_in(key, 1), 0)
    values = jax.random.truncated_normal(base_key, -4.0, 4.0, (LENGTH, LENGTH, CZ), jnp.float32)
    return values.astype(jnp.bfloat16)


def draw_seq_state(key, part):
    base_key = jax.random.fold_in(jax.random.fold_in(key, 2), 0)
    values = jax.random.truncated_normal(base_key, -4.0, 4.0, (LENGTH, CS), jnp.float32)
    return values.astype(jnp.bfloat16)


def attention_pair(key):
    key_first, key_second = jax.random.split(jax.random.fold_in(key, 7), 2)
    shaped = (LAYERS, CS, CS)
    key_part = jax.random.truncated_normal(key_first, -4.0, 4.0, shaped, jnp.float32) * CS ** (-0.5)
    noise_part = jax.random.truncated_normal(key_second, -4.0, 4.0, shaped, jnp.float32) * CS ** (-0.5)
    return (key_part, noise_part)


def draw_key_weight(key, part):
    key_part, noise_part = attention_pair(key)
    return key_part.astype(jnp.bfloat16)


def draw_query_weight(key, part):
    key_part, noise_part = attention_pair(key)
    return noise_part.astype(jnp.bfloat16)


def draw_residue_mask(key, part):
    live_count = jax.random.randint(jax.random.fold_in(key, 3), (), LENGTH // 2, LENGTH)
    return (jnp.arange(LENGTH, dtype=jnp.int32) < live_count).astype(jnp.int32)


def draw_residue_index(key, part):
    inner_count = 4 * LENGTH - 2
    chosen = jax.random.permutation(jax.random.fold_in(key, 5), inner_count)[:LENGTH - 2].astype(jnp.int32) + 1
    ends = jnp.array([0, 4 * LENGTH - 1], dtype=jnp.int32)
    return jnp.sort(jnp.concatenate([ends, chosen])).astype(jnp.int32)


def block_levels(own_key, extent, shards, smallest, largest):
    def one(position, blocks):
        heights = jax.random.uniform(jax.random.fold_in(jax.random.fold_in(own_key, 6), position), (blocks,), jnp.float32, smallest / len(shards), largest / len(shards))
        return jnp.repeat(jnp.exp(heights), extent[position] // blocks).reshape((-1,) + (1,) * (len(extent) - position - 1))

    gain = one(*shards[0])
    for cut in shards[1:]:
        gain = gain * one(*cut)
    return gain


def bell_draw(own_key, extent, deviation, most, pieces=(), kind=jnp.bfloat16):
    gain = block_levels(own_key, extent, pieces, -0.22, 0.18) if pieces else 1.0
    values = jax.random.normal(own_key, extent, jnp.float32) * deviation * gain
    return jnp.minimum(jnp.maximum(values, -most), most).astype(kind)


def setup_inputs(seed: int = 0) -> dict:
    arg_keys = jax.random.split(jax.random.key(seed), 21)
    return {
        "pair_state": draw_pair_state(jax.random.fold_in(arg_keys[20], 71), 0),
        "seq_state": draw_seq_state(jax.random.fold_in(arg_keys[20], 71), 0),
        "residue_index": draw_residue_index(jax.random.fold_in(arg_keys[20], 71), 0),
        "residue_mask": draw_residue_mask(jax.random.fold_in(arg_keys[20], 71), 0),
        "position_table": bell_draw(arg_keys[4], (RELPOS_BINS, CZ), 1.0, 4.0),
        "attention_gain": jnp.clip(1.0 + 0.18 * jax.random.normal(arg_keys[5], (LAYERS, CS), jnp.float32), 0.1, 1.9),
        "bias_norm_gain": jnp.clip(1.0 + 0.18 * jax.random.normal(arg_keys[6], (LAYERS, CZ), jnp.float32), 0.1, 1.9),
        "query_weight": draw_query_weight(jax.random.fold_in(arg_keys[20], 71), 0),
        "key_weight": draw_key_weight(jax.random.fold_in(arg_keys[20], 71), 0),
        "value_weight": bell_draw(arg_keys[9], (LAYERS, CS, CS), CS ** -0.5, 0.1875, ((2, 8),)),
        "gate_weight": bell_draw(arg_keys[10], (LAYERS, CS, CS), CS ** -0.5, 0.1875, ((2, 8),)),
        "out_weight": bell_draw(arg_keys[11], (LAYERS, CS, CS), (CS // 16) ** -0.5, 0.75, ((2, 8),)),
        "bias_weight": bell_draw(arg_keys[12], (LAYERS, CZ, HEADS), (CZ // 9) ** -0.5, 1.5),
        "outer_gain": jnp.clip(1.0 + 0.18 * jax.random.normal(arg_keys[13], (LAYERS, CS), jnp.float32), 0.1, 1.9),
        "outer_weight": bell_draw(arg_keys[14], (LAYERS, CS, 2 * INNER), CS ** -0.5, 0.1875),
        "outer_out_weight": bell_draw(arg_keys[15], (LAYERS, 2 * INNER, CZ), (2 * INNER) ** -0.5, 0.5),
        "transition_gain": jnp.clip(1.0 + 0.18 * jax.random.normal(arg_keys[16], (LAYERS, CZ), jnp.float32), 0.1, 1.9),
        "up_weight": bell_draw(arg_keys[17], (LAYERS, CZ, FFZ), CZ ** -0.5, 0.5),
        "down_weight": bell_draw(arg_keys[18], (LAYERS, FFZ, CZ), FFZ ** -0.5, 0.25),
        "distance_weight": bell_draw(arg_keys[19], (CZ, BINS), CZ ** -0.5, 0.5),
    }


def normalize(values, weight_gain):
    average = lax.optimization_barrier(jnp.mean(values, axis=-1, keepdims=True))
    centred = values - average
    spread = lax.optimization_barrier(jnp.mean(centred * centred, axis=-1, keepdims=True))
    return centred * lax.rsqrt(spread + 1e-05) * weight_gain.astype(jnp.float32)

def settle(values):
    rounded = lax.optimization_barrier(values.astype(jnp.bfloat16))
    return rounded.astype(jnp.float32)

def reference(pair_state, seq_state, residue_index, residue_mask, position_table, attention_gain, bias_norm_gain, query_weight, key_weight, value_weight, gate_weight, out_weight, bias_weight, outer_gain, outer_weight, outer_out_weight, transition_gain, up_weight, down_weight, distance_weight):
    length = seq_state.shape[0]
    blocks = N_ROW
    block_rows = length // blocks
    live_mask = residue_mask > 0
    pair_live = live_mask[:, None] & live_mask[None, :]
    offset = jnp.clip(residue_index[None, :] - residue_index[:, None], -RELPOS_MAX, RELPOS_MAX) + RELPOS_MAX + 1
    bin_index = jnp.where(pair_live, offset, 0).astype(jnp.int32)
    pair_now = pair_state.astype(jnp.float32) + position_table.astype(jnp.float32)[bin_index]
    seq_now = seq_state
    score_scale = HEAD_DIM ** (-0.5)
    for layer_index in range(LAYERS):
        normed_seq = normalize(seq_now.astype(jnp.float32), attention_gain[layer_index]).astype(jnp.bfloat16)
        queries = (jnp.dot(normed_seq, query_weight[layer_index], preferred_element_type=jnp.float32) * score_scale).astype(jnp.bfloat16)
        keys_local = jnp.dot(normed_seq, key_weight[layer_index], preferred_element_type=jnp.float32).astype(jnp.bfloat16)
        values_local = jnp.dot(normed_seq, value_weight[layer_index], preferred_element_type=jnp.float32).astype(jnp.bfloat16)
        gating = jax.nn.sigmoid(jnp.dot(normed_seq, gate_weight[layer_index], preferred_element_type=jnp.float32))

        def bias_block(pair_tile):
            normed_pair = normalize(pair_tile, bias_norm_gain[layer_index]).astype(jnp.bfloat16)
            return jnp.einsum('ijc,ch->hij', normed_pair.astype(jnp.float32), bias_weight[layer_index].astype(jnp.float32)).astype(jnp.bfloat16)
        pair_bias = lax.map(bias_block, pair_now.reshape(blocks, block_rows, length, CZ))
        pair_bias = jnp.transpose(pair_bias, (1, 0, 2, 3)).reshape(HEADS, length, length)
        head_query = jnp.transpose(queries.reshape(length, HEADS, HEAD_DIM), (1, 0, 2))
        head_key = jnp.transpose(keys_local.reshape(length, HEADS, HEAD_DIM), (1, 0, 2))
        head_value = jnp.transpose(values_local.reshape(length, HEADS, HEAD_DIM), (1, 0, 2))

        def attend(inputs):
            one_query, one_key, one_value, one_bias = inputs
            scores = jnp.dot(one_query, one_key.T, preferred_element_type=jnp.float32) + one_bias.astype(jnp.float32)
            scores = jnp.where(live_mask[None, :], scores, -jnp.inf)
            row_max = lax.optimization_barrier(jnp.max(scores, axis=-1, keepdims=True))
            shifted = jnp.exp(scores - row_max)
            weights = (shifted / lax.optimization_barrier(jnp.sum(shifted, axis=-1, keepdims=True))).astype(jnp.bfloat16)
            return jnp.dot(weights, one_value, preferred_element_type=jnp.float32)
        attended = lax.map(attend, (head_query, head_key, head_value, pair_bias))
        attended = jnp.transpose(attended, (1, 0, 2)).reshape(length, CS)
        gated_out = (gating * attended).astype(jnp.bfloat16)
        seq_now = (seq_now.astype(jnp.float32) + jnp.dot(gated_out, out_weight[layer_index], preferred_element_type=jnp.float32)).astype(jnp.bfloat16)
        outer_in = normalize(seq_now.astype(jnp.float32), outer_gain[layer_index]).astype(jnp.bfloat16)
        projected = jnp.dot(outer_in, outer_weight[layer_index], preferred_element_type=jnp.float32)
        left_side = projected[:, :INNER].astype(jnp.bfloat16)
        right_wide = projected[:, INNER:].astype(jnp.bfloat16).astype(jnp.float32)[None, :, :]

        def pair_block(inputs):
            pair_tile, left_rows = inputs
            left_wide = left_rows.astype(jnp.float32)[:, None, :]
            features = jnp.concatenate([left_wide * right_wide, left_wide - right_wide], axis=-1).astype(jnp.bfloat16)
            pair_mid = pair_tile + jnp.dot(features.reshape(-1, 2 * INNER), outer_out_weight[layer_index], preferred_element_type=jnp.float32).reshape(pair_tile.shape)
            normed_pair = normalize(pair_mid, transition_gain[layer_index]).astype(jnp.bfloat16)
            hidden = jax.nn.relu(jnp.dot(normed_pair.reshape(-1, CZ), up_weight[layer_index], preferred_element_type=jnp.float32)).astype(jnp.bfloat16)
            return settle(pair_mid + jnp.dot(hidden, down_weight[layer_index], preferred_element_type=jnp.float32).reshape(pair_tile.shape))
        pair_now = lax.map(pair_block, (pair_now.reshape(blocks, block_rows, length, CZ), left_side.reshape(blocks, block_rows, INNER))).reshape(length, length, CZ)
    final_pair = pair_now.astype(jnp.bfloat16)

    def logit_block(pair_tile):
        return jnp.dot(pair_tile.reshape(-1, CZ), distance_weight, preferred_element_type=jnp.float32).astype(jnp.bfloat16).reshape(pair_tile.shape[0], length, BINS)
    logits = lax.map(logit_block, final_pair.reshape(blocks, block_rows, length, CZ)).reshape(length, length, BINS)
    mirrored = jnp.transpose(logits, (1, 0, 2))
    distogram = ((logits.astype(jnp.float32) + mirrored.astype(jnp.float32)) * 0.5).astype(jnp.bfloat16)
    return (distogram, seq_now)
```

```python
import jax
import jax.numpy as jnp
from jax import lax
from jax.experimental import pallas as pl
from jax.experimental.pallas import tpu as pltpu
from jax.sharding import PartitionSpec as P

HEAD_DIM = 32
RELPOS_MAX = 32
MESH = pl.DeviceIdType.MESH


def normalize(values, weight_gain):
    average = jnp.mean(values, axis=-1, keepdims=True)
    centred = values - average
    spread = jnp.mean(centred * centred, axis=-1, keepdims=True)
    return centred * lax.rsqrt(spread + 1e-05) * weight_gain


def settle(values):
    rounded = lax.optimization_barrier(values.astype(jnp.bfloat16))
    return rounded.astype(jnp.float32)


def gather(block, axis, own_id):
    total = lax.axis_size(axis)

    def kernel(block_ref, out_ref, send_sem, recv_sem, local_sem):
        me = lax.axis_index(axis)
        barrier = pltpu.get_barrier_semaphore()
        for step in range(1, total):
            pl.semaphore_signal(
                barrier, inc=1, device_id={axis: lax.rem(me + step, total)}, device_id_type=MESH
            )
        pl.semaphore_wait(barrier, total - 1)
        copies = []
        for step in range(1, total):
            copies.append(
                pltpu.make_async_remote_copy(
                    src_ref=block_ref,
                    dst_ref=out_ref.at[me],
                    send_sem=send_sem.at[step - 1],
                    recv_sem=recv_sem.at[step - 1],
                    device_id={axis: lax.rem(me + step, total)},
                    device_id_type=MESH,
                )
            )
        for copy in copies:
            copy.start()
        own = pltpu.make_async_copy(block_ref, out_ref.at[me], local_sem)
        own.start()
        own.wait()
        for copy in copies:
            copy.wait()

    return pl.pallas_call(
        kernel,
        out_shape=jax.ShapeDtypeStruct((total,) + block.shape, block.dtype),
        in_specs=[pl.BlockSpec(memory_space=pltpu.VMEM)],
        out_specs=pl.BlockSpec(memory_space=pltpu.VMEM),
        scratch_shapes=[
            pltpu.SemaphoreType.DMA((total - 1,)),
            pltpu.SemaphoreType.DMA((total - 1,)),
            pltpu.SemaphoreType.DMA,
        ],
        compiler_params=pltpu.CompilerParams(collective_id=own_id, has_side_effects=True),
    )(block)


def gather_lanes(block, axis, own_id):
    stacked = gather(block, axis, own_id)
    return jnp.transpose(stacked, (1, 0, 2)).reshape(block.shape[0], -1)


def gather_rows(block, axis, own_id):
    return gather(block, axis, own_id).reshape(-1, block.shape[1])


def mirror(logit_tile, own_id):
    tile_rows, tile_cols, bin_count = logit_tile.shape
    parts = tile_rows // tile_cols
    flat = logit_tile.reshape(parts, tile_cols * tile_cols * bin_count // 128, 128)

    def kernel(flat_ref, out_ref, send_sem, recv_sem, local_sem):
        row, col = lax.axis_index("row"), lax.axis_index("col")
        peer_row, slot = lax.div(col, parts), lax.rem(col, parts)
        barrier = pltpu.get_barrier_semaphore()
        on_diagonal = peer_row == row
        for part in range(parts):
            same = jnp.logical_and(on_diagonal, slot == part)

            @pl.when(jnp.logical_not(same))
            def _(part=part):
                pl.semaphore_signal(
                    barrier,
                    inc=1,
                    device_id={"row": peer_row, "col": row * parts + part},
                    device_id_type=MESH,
                )

        pl.semaphore_wait(barrier, jnp.where(on_diagonal, parts - 1, parts))
        for part in range(parts):
            same = jnp.logical_and(on_diagonal, slot == part)
            away = pltpu.make_async_remote_copy(
                src_ref=flat_ref.at[part],
                dst_ref=out_ref.at[slot],
                send_sem=send_sem.at[part],
                recv_sem=recv_sem.at[slot],
                device_id={"row": peer_row, "col": row * parts + part},
                device_id_type=MESH,
            )
            stay = pltpu.make_async_copy(flat_ref.at[part], out_ref.at[part], local_sem)
            pl.when(jnp.logical_not(same))(away.start)
            pl.when(same)(stay.start)
        for part in range(parts):
            same = jnp.logical_and(on_diagonal, slot == part)
            away = pltpu.make_async_remote_copy(
                src_ref=flat_ref.at[part],
                dst_ref=out_ref.at[part],
                send_sem=send_sem.at[part],
                recv_sem=recv_sem.at[part],
                device_id={"row": peer_row, "col": row * parts + part},
                device_id_type=MESH,
            )
            stay = pltpu.make_async_copy(flat_ref.at[part], out_ref.at[part], local_sem)
            pl.when(jnp.logical_not(same))(away.wait)
            pl.when(same)(stay.wait)

    moved = pl.pallas_call(
        kernel,
        out_shape=jax.ShapeDtypeStruct(flat.shape, flat.dtype),
        in_specs=[pl.BlockSpec(memory_space=pltpu.VMEM)],
        out_specs=pl.BlockSpec(memory_space=pltpu.VMEM),
        scratch_shapes=[
            pltpu.SemaphoreType.DMA((parts,)),
            pltpu.SemaphoreType.DMA((parts,)),
            pltpu.SemaphoreType.DMA,
        ],
        compiler_params=pltpu.CompilerParams(collective_id=own_id, has_side_effects=True),
    )(flat)
    moved = moved.reshape(parts, tile_cols, tile_cols, bin_count)
    return jnp.transpose(moved, (0, 2, 1, 3)).reshape(tile_rows, tile_cols, bin_count)


def per_device(
    pair_state,
    seq_state,
    residue_index,
    residue_mask,
    position_table,
    attention_gain,
    bias_norm_gain,
    query_weight,
    key_weight,
    value_weight,
    gate_weight,
    out_weight,
    bias_weight,
    outer_gain,
    outer_weight,
    outer_out_weight,
    transition_gain,
    up_weight,
    down_weight,
    distance_weight,
):
    col_total = lax.axis_size("col")
    tile_rows, tile_cols, channels = pair_state.shape
    length = tile_cols * col_total
    row_first = lax.axis_index("row") * tile_rows
    col_first = lax.axis_index("col") * tile_cols
    row_pos = lax.dynamic_slice_in_dim(residue_index, row_first, tile_rows)
    col_pos = lax.dynamic_slice_in_dim(residue_index, col_first, tile_cols)
    row_live = lax.dynamic_slice_in_dim(residue_mask, row_first, tile_rows) > 0
    col_live = lax.dynamic_slice_in_dim(residue_mask, col_first, tile_cols) > 0
    key_live = residue_mask > 0
    offset = jnp.clip(col_pos[None, :] - row_pos[:, None], -RELPOS_MAX, RELPOS_MAX) + RELPOS_MAX + 1
    bin_index = jnp.where(row_live[:, None] & col_live[None, :], offset, 0)
    table_rows = position_table.shape[0]
    padded_rows = (table_rows + 127) // 128 * 128
    table_padded = jnp.pad(position_table, ((0, padded_rows - table_rows), (0, 0)))
    one_hot = (
        bin_index.reshape(-1, 1) == jnp.arange(padded_rows, dtype=jnp.int32)[None, :]
    ).astype(jnp.bfloat16)
    pair_now = pair_state.astype(jnp.float32) + jnp.dot(
        one_hot, table_padded, preferred_element_type=jnp.float32
    ).reshape(tile_rows, tile_cols, channels)
    head_width = query_weight.shape[2]
    local_heads = head_width // HEAD_DIM
    score_scale = HEAD_DIM ** (-0.5)
    seq_now = seq_state
    for layer_index in range(query_weight.shape[0]):
        if layer_index == 0:
            seq_full = gather_lanes(seq_now, "col", 0)
        normed_seq = normalize(seq_full.astype(jnp.float32), attention_gain[layer_index]).astype(
            jnp.bfloat16
        )
        queries = (
            jnp.dot(normed_seq, query_weight[layer_index], preferred_element_type=jnp.float32)
            * score_scale
        ).astype(jnp.bfloat16)
        keys_local = jnp.dot(
            normed_seq, key_weight[layer_index], preferred_element_type=jnp.float32
        ).astype(jnp.bfloat16)
        values_local = jnp.dot(
            normed_seq, value_weight[layer_index], preferred_element_type=jnp.float32
        ).astype(jnp.bfloat16)
        gating = jax.nn.sigmoid(
            jnp.dot(normed_seq, gate_weight[layer_index], preferred_element_type=jnp.float32)
        )
        both_all = gather_rows(
            jnp.concatenate([keys_local, values_local], axis=1), "row", 4 * layer_index + 1
        )
        keys_all, values_all = both_all[:, :head_width], both_all[:, head_width:]
        normed_pair = normalize(pair_now, bias_norm_gain[layer_index]).astype(jnp.bfloat16)
        pair_bias = jnp.einsum(
            "ijc,ch->hij", normed_pair, bias_weight[layer_index], preferred_element_type=jnp.float32
        ).astype(jnp.bfloat16)
        head_bias = lax.all_to_all(pair_bias, "col", split_axis=0, concat_axis=2, tiled=True)
        scores = jnp.einsum(
            "qhd,khd->hqk",
            queries.reshape(tile_rows, local_heads, HEAD_DIM),
            keys_all.reshape(length, local_heads, HEAD_DIM),
            preferred_element_type=jnp.float32,
        )
        scores = jnp.where(
            key_live[None, None, :], scores + head_bias.astype(jnp.float32), -jnp.inf
        )
        row_max = jnp.max(scores, axis=-1, keepdims=True)
        shifted = jnp.exp(scores - row_max)
        weights = (shifted / jnp.sum(shifted, axis=-1, keepdims=True)).astype(jnp.bfloat16)
        attended = jnp.einsum(
            "hqk,khd->qhd",
            weights,
            values_all.reshape(length, local_heads, HEAD_DIM),
            preferred_element_type=jnp.float32,
        ).reshape(tile_rows, head_width)
        gated_out = (gating * attended).astype(jnp.bfloat16)
        out_layer = out_weight[layer_index]
        update_seq = jnp.dot(
            gather_lanes(gated_out, "col", 4 * layer_index + 2),
            out_layer,
            preferred_element_type=jnp.float32,
        )
        seq_now = (seq_now.astype(jnp.float32) + update_seq).astype(jnp.bfloat16)
        seq_full = gather_lanes(seq_now, "col", 4 * layer_index + 3)
        outer_in = normalize(seq_full.astype(jnp.float32), outer_gain[layer_index]).astype(
            jnp.bfloat16
        )
        projected = jnp.dot(outer_in, outer_weight[layer_index], preferred_element_type=jnp.float32)
        inner_width = projected.shape[1] // 2
        left_side = projected[:, :inner_width].astype(jnp.bfloat16)
        right_side = projected[:, inner_width:].astype(jnp.bfloat16)
        right_all = gather_rows(right_side, "row", 4 * layer_index + 4)
        right_cols = lax.dynamic_slice_in_dim(right_all, col_first, tile_cols, 0)
        left_wide = left_side.astype(jnp.float32)[:, None, :]
        right_wide = right_cols.astype(jnp.float32)[None, :, :]
        features = jnp.concatenate(
            [left_wide * right_wide, left_wide - right_wide], axis=-1
        ).astype(jnp.bfloat16)
        pair_now = pair_now + jnp.dot(
            features.reshape(-1, 2 * inner_width),
            outer_out_weight[layer_index],
            preferred_element_type=jnp.float32,
        ).reshape(tile_rows, tile_cols, channels)
        normed_pair = normalize(pair_now, transition_gain[layer_index]).astype(jnp.bfloat16)
        hidden = jax.nn.relu(
            jnp.dot(
                normed_pair.reshape(-1, channels),
                up_weight[layer_index],
                preferred_element_type=jnp.float32,
            )
        ).astype(jnp.bfloat16)
        pair_now = settle(
            pair_now
            + jnp.dot(hidden, down_weight[layer_index], preferred_element_type=jnp.float32).reshape(
                tile_rows, tile_cols, channels
            )
        )
    final_pair = pair_now.astype(jnp.bfloat16)
    logits = (
        jnp.dot(
            final_pair.reshape(-1, channels), distance_weight, preferred_element_type=jnp.float32
        )
        .astype(jnp.bfloat16)
        .reshape(tile_rows, tile_cols, distance_weight.shape[1])
    )
    mirrored = mirror(logits, 9)
    distogram = ((logits.astype(jnp.float32) + mirrored.astype(jnp.float32)) * 0.5).astype(
        jnp.bfloat16
    )
    return (distogram, seq_now)


def solution(mesh):
    in_specs = (
        P("row", "col", None),
        P("row", "col"),
        P(),
        P(),
        P(),
        P(),
        P(),
        P(None, None, "col"),
        P(None, None, "col"),
        P(None, None, "col"),
        P(None, None, "col"),
        P(None, None, "col"),
        P(),
        P(),
        P(),
        P(),
        P(),
        P(),
        P(),
        P(),
    )
    out_specs = (P("row", "col", None), P("row", "col"))
    return jax.shard_map(
        per_device, mesh=mesh, in_specs=in_specs, out_specs=out_specs, check_vma=False
    )
```

```python
import jax
import jax.numpy as jnp
from jax import lax
from jax.experimental import pallas as pl
from jax.experimental.pallas import tpu as pltpu
from jax.sharding import PartitionSpec as P

HEAD_DIM = 32
RELPOS_MAX = 32
MESH = pl.DeviceIdType.MESH


def normalize(values, weight_gain):
    average = jnp.mean(values, axis=-1, keepdims=True)
    centred = values - average
    spread = jnp.mean(centred * centred, axis=-1, keepdims=True)
    return centred * lax.rsqrt(spread + 1e-05) * weight_gain


def full_spec():
    return pl.BlockSpec(memory_space=pltpu.VMEM)


def lane_join(stacked_ref):
    return jnp.concatenate([stacked_ref[k] for k in range(stacked_ref.shape[0])], axis=1)


def spread(source, target, axis, send_sem, recv_sem):
    total, me = lax.axis_size(axis), lax.axis_index(axis)
    copies = []
    for step in range(1, total):
        peer = lax.rem(me + step, total)
        copies.append(
            pltpu.make_async_remote_copy(
                src_ref=source(peer),
                dst_ref=target(me),
                send_sem=send_sem.at[step - 1],
                recv_sem=recv_sem.at[step - 1],
                device_id={axis: peer},
                device_id_type=MESH,
            )
        )
    for copy in copies:
        copy.start()
    return copies


def finish(copies):
    for copy in copies:
        copy.wait()


def sequence_step(
    layer, seq_tile, seq_all, bias_send, live_column, gains, weights, outer_weight, own_id
):
    nr, nc = lax.axis_size("row"), lax.axis_size("col")
    tr, width = seq_tile.shape
    heads, tc, lanes = bias_send.shape
    hl = heads // nc
    length = nr * tr
    cs = outer_weight.shape[1]
    wide = outer_weight.shape[2]
    first = seq_all is None
    score_scale = HEAD_DIM ** (-0.5)

    def kernel(*refs):
        it = iter(refs)
        seq_ref = next(it)
        seq_all_ref = None if first else next(it)
        bias_ref, live_ref, gain_ref, outer_gain_ref = (next(it) for _ in range(4))
        weight_hbm = [next(it) for _ in range(6)]
        seq_out, seq_out_all, proj_all = (next(it) for _ in range(3))
        weight_refs = [next(it) for _ in range(6)]
        gathered, kv_all, bias_all, gated_all = (next(it) for _ in range(4))
        weight_sem = next(it)
        col_send, col_recv, row_send, row_recv = (next(it) for _ in range(4))

        loads = [
            pltpu.make_async_copy(weight_hbm[k].at[layer], weight_refs[k], weight_sem.at[k])
            for k in range(6)
        ]
        for load in loads:
            load.start()
        row, col = lax.axis_index("row"), lax.axis_index("col")
        barrier = pltpu.get_barrier_semaphore()
        for axis, total, me in (("col", nc, col), ("row", nr, row)):
            for step in range(1, total):
                pl.semaphore_signal(
                    barrier,
                    inc=1,
                    device_id={axis: lax.rem(me + step, total)},
                    device_id_type=MESH,
                )
        pl.semaphore_wait(barrier, nc + nr - 2)
        if first:
            seq_copies = spread(
                lambda peer: seq_ref,
                lambda me: gathered.at[me],
                "col",
                col_send.at[0],
                col_recv.at[0],
            )
        bias_copies = spread(
            lambda peer: bias_ref.at[pl.ds(peer * hl, hl)],
            lambda me: bias_all.at[me],
            "col",
            col_send.at[1],
            col_recv.at[1],
        )
        bias_all[col] = bias_ref[pl.ds(col * hl, hl)]
        if first:
            gathered[col] = seq_ref[...]
            finish(seq_copies)
            entering = lane_join(gathered)
        else:
            entering = lane_join(seq_all_ref)
        normed = normalize(entering.astype(jnp.float32), gain_ref[pl.ds(layer, 1), :]).astype(
            jnp.bfloat16
        )

        def product(value, k):
            return jnp.dot(value, weight_refs[k][...], preferred_element_type=jnp.float32)

        loads[1].wait()
        kv_all[row, 0] = product(normed, 1).astype(jnp.bfloat16)
        loads[2].wait()
        kv_all[row, 1] = product(normed, 2).astype(jnp.bfloat16)
        kv_copies = spread(
            lambda peer: kv_all.at[row],
            lambda me: kv_all.at[me],
            "row",
            row_send.at[0],
            row_recv.at[0],
        )
        loads[0].wait()
        queries = (product(normed, 0) * score_scale).astype(jnp.bfloat16)
        loads[3].wait()
        gating = jax.nn.sigmoid(product(normed, 3))
        head_of = lax.broadcasted_iota(jnp.int32, (tr, width), 1) // HEAD_DIM
        finish(kv_copies)
        finish(bias_copies)
        keys = kv_all[:, 0].reshape(length, width)
        values = kv_all[:, 1].reshape(length, width)
        live = live_ref[...] > 0
        attended = jnp.zeros((tr, width), jnp.float32)
        for head in range(hl):
            own = head_of == head
            query = jnp.where(own, queries.astype(jnp.float32), 0.0).astype(jnp.bfloat16)
            scores = lax.dot_general(
                keys, query, (((1,), (1,)), ((), ())), preferred_element_type=jnp.float32
            )
            bias = bias_all[:, head].reshape(length, lanes)[:, :tr]
            scores = jnp.where(live, scores + bias.astype(jnp.float32), -jnp.inf)
            shifted = jnp.exp(scores - jnp.max(scores, axis=0, keepdims=True))
            share = (shifted / jnp.sum(shifted, axis=0, keepdims=True)).astype(jnp.bfloat16)
            mixed = lax.dot_general(
                share, values, (((0,), (0,)), ((), ())), preferred_element_type=jnp.float32
            )
            attended = jnp.where(own, mixed, attended)
        gated_all[col] = (gating * attended).astype(jnp.bfloat16)
        finish(
            spread(
                lambda peer: gated_all.at[col],
                lambda me: gated_all.at[me],
                "col",
                col_send.at[2],
                col_recv.at[2],
            )
        )
        loads[4].wait()
        leaving = (seq_ref[...].astype(jnp.float32) + product(lane_join(gated_all), 4)).astype(
            jnp.bfloat16
        )
        seq_out_all[col] = leaving
        seq_out[...] = leaving
        finish(
            spread(
                lambda peer: seq_out_all.at[col],
                lambda me: seq_out_all.at[me],
                "col",
                col_send.at[3],
                col_recv.at[3],
            )
        )
        outer_in = normalize(
            lane_join(seq_out_all).astype(jnp.float32), outer_gain_ref[pl.ds(layer, 1), :]
        ).astype(jnp.bfloat16)
        loads[5].wait()
        proj_all[row] = product(outer_in, 5).astype(jnp.bfloat16)
        finish(
            spread(
                lambda peer: proj_all.at[row],
                lambda me: proj_all.at[me],
                "row",
                row_send.at[1],
                row_recv.at[1],
            )
        )

    operands = [seq_tile] + ([] if first else [seq_all]) + [bias_send, live_column, *gains]
    specs = [full_spec()] * len(operands) + [pl.BlockSpec(memory_space=pl.ANY)] * 6
    bf16 = jnp.bfloat16
    return pl.pallas_call(
        kernel,
        out_shape=(
            jax.ShapeDtypeStruct((tr, width), bf16),
            jax.ShapeDtypeStruct((nc, tr, width), bf16),
            jax.ShapeDtypeStruct((nr, tr, wide), bf16),
        ),
        in_specs=specs,
        out_specs=(full_spec(),) * 3,
        scratch_shapes=[pltpu.VMEM((cs, width), bf16)] * 5
        + [
            pltpu.VMEM((cs, wide), bf16),
            pltpu.VMEM((nc, tr, width), bf16),
            pltpu.VMEM((nr, 2, tr, width), bf16),
            pltpu.VMEM((nc, hl, tc, lanes), bf16),
            pltpu.VMEM((nc, tr, width), bf16),
            pltpu.SemaphoreType.DMA((6,)),
            pltpu.SemaphoreType.DMA((4, nc - 1)),
            pltpu.SemaphoreType.DMA((4, nc - 1)),
            pltpu.SemaphoreType.DMA((2, nr - 1)),
            pltpu.SemaphoreType.DMA((2, nr - 1)),
        ],
        compiler_params=pltpu.CompilerParams(collective_id=own_id, has_side_effects=True),
    )(*operands, *weights, outer_weight)


def bias_rows(pair_ref, gain, weight, mixed_ref, out_ref, tr, tc):
    heads = weight.shape[0]

    @pl.loop(0, tc, unroll=4)
    def _(j):
        normed = normalize(pair_ref[pl.ds(j, tr, stride=tc), :], gain).astype(jnp.bfloat16)
        mixed_ref[pl.ds(j * heads, heads), 0:tr] = lax.dot_general(
            weight, normed, (((1,), (1,)), ((), ())), preferred_element_type=jnp.float32
        )

    for head in range(heads):
        out_ref[head] = mixed_ref[pl.ds(head, tc, stride=heads), :].astype(jnp.bfloat16)


def bias_step(layer, pair_flat, tr, tc, bias_norm_gain, bias_weight_t):
    heads = bias_weight_t.shape[1]
    lanes = (tr + 127) // 128 * 128

    def kernel(pair_ref, gain_ref, weight_ref, out_ref, mixed_ref):
        bias_rows(pair_ref, gain_ref[pl.ds(layer, 1), :], weight_ref[layer], mixed_ref, out_ref, tr, tc)

    return pl.pallas_call(
        kernel,
        out_shape=jax.ShapeDtypeStruct((heads, tc, lanes), jnp.bfloat16),
        in_specs=[full_spec()] * 3,
        out_specs=full_spec(),
        scratch_shapes=[pltpu.VMEM((tc * heads, lanes), jnp.float32)],
    )(pair_flat, bias_norm_gain, bias_weight_t)


def pair_step(layer, last, pair_flat, proj_all, tr, tc, mats, gains, bias_weight_t, heads_of_bins):
    channels = pair_flat.shape[1]
    heads = bias_weight_t.shape[1]
    lanes = (tr + 127) // 128 * 128
    rows = 8
    parts = tr // tc
    half = tc // 2

    def kernel(
        pair_ref,
        proj_ref,
        outer_ref,
        up_ref,
        down_ref,
        transition_ref,
        bias_gain_ref,
        bias_weight_ref,
        bins_ref,
        out_ref,
        extra_ref,
        fresh_ref,
        mixed_ref,
        left_ref,
    ):
        row, col = lax.axis_index("row"), lax.axis_index("col")
        low = lax.broadcasted_iota(jnp.int32, (1, channels), 1) < channels // 2
        left = proj_ref[pl.ds(pl.multiple_of(row * tr, 16), tr), :].astype(jnp.float32)
        left_ref[...] = jnp.where(low, left, pltpu.roll(left, channels // 2, axis=1))
        right = proj_ref[pl.ds(pl.multiple_of(col * tc, 16), tc), :].astype(jnp.float32)
        right = jnp.where(low, pltpu.roll(right, channels // 2, axis=1), right)[None]
        gain = transition_ref[pl.ds(layer, 1), :]

        @pl.loop(0, tr // rows)
        def _(step):
            at = pl.ds(pl.multiple_of(step * (rows * tc), rows * tc), rows * tc)
            left = left_ref[pl.ds(pl.multiple_of(step * rows, rows), rows), :][:, None, :]
            features = jnp.where(low[None], left * right, left - right)
            features = features.reshape(rows * tc, channels).astype(jnp.bfloat16)
            middle = pair_ref[at, :].astype(jnp.float32) + jnp.dot(
                features, outer_ref[layer], preferred_element_type=jnp.float32
            )
            normed = normalize(middle, gain).astype(jnp.bfloat16)
            hidden = jnp.maximum(
                jnp.dot(normed, up_ref[layer], preferred_element_type=jnp.float32), 0.0
            ).astype(jnp.bfloat16)
            fresh = (
                middle + jnp.dot(hidden, down_ref[layer], preferred_element_type=jnp.float32)
            ).astype(jnp.bfloat16)
            if last:
                fresh_ref[at, :] = fresh.astype(jnp.float32)
                out_ref[at, :] = jnp.dot(
                    fresh, bins_ref[0], preferred_element_type=jnp.float32
                ).astype(jnp.bfloat16)
            else:
                out_ref[at, :] = fresh
                fresh_ref[at, :] = fresh.astype(jnp.float32)

        if last:
            count = half * tc
            for part in range(parts):
                near = fresh_ref[pl.ds(part * 2 * count, count), :].astype(jnp.bfloat16)
                far = fresh_ref[pl.ds((part * 2 + 1) * count, count), :].astype(jnp.bfloat16)
                extra_ref[part] = (
                    jnp.dot(near, bins_ref[0], preferred_element_type=jnp.float32)
                    + jnp.dot(far, bins_ref[1], preferred_element_type=jnp.float32)
                ).astype(jnp.bfloat16)
        else:
            bias_rows(
                fresh_ref,
                bias_gain_ref[pl.ds(layer + 1, 1), :],
                bias_weight_ref[layer + 1],
                mixed_ref,
                extra_ref,
                tr,
                tc,
            )

    width = heads_of_bins.shape[2]
    extra = (parts, half * tc, width) if last else (heads, tc, lanes)
    operands = (pair_flat, proj_all, *mats, *gains, bias_weight_t, heads_of_bins)
    return pl.pallas_call(
        kernel,
        out_shape=(
            jax.ShapeDtypeStruct((tr * tc, width if last else channels), jnp.bfloat16),
            jax.ShapeDtypeStruct(extra, jnp.bfloat16),
        ),
        in_specs=[full_spec()] * len(operands),
        out_specs=(full_spec(),) * 2,
        scratch_shapes=[
            pltpu.VMEM((tr * tc, channels), jnp.float32),
            pltpu.VMEM((tc * heads, lanes), jnp.float32),
            pltpu.VMEM((tr, channels), jnp.float32),
        ],
    )(*operands)


def mirror(logit_flat, flat, tile_rows, tile_cols, bin_count, own_id):
    parts = tile_rows // tile_cols
    half = tile_cols // 2

    def kernel(flat_ref, logit_ref, final_ref, out_ref, wide_ref, send_sem, recv_sem, local_sem):
        row, col = lax.axis_index("row"), lax.axis_index("col")
        peer_row, slot = lax.div(col, parts), lax.rem(col, parts)
        barrier = pltpu.get_barrier_semaphore()
        on_diagonal = peer_row == row
        for part in range(parts):
            same = jnp.logical_and(on_diagonal, slot == part)

            @pl.when(jnp.logical_not(same))
            def _(part=part):
                pl.semaphore_signal(
                    barrier,
                    inc=1,
                    device_id={"row": peer_row, "col": row * parts + part},
                    device_id_type=MESH,
                )

        pl.semaphore_wait(barrier, jnp.where(on_diagonal, parts - 1, parts))
        for part in range(parts):
            same = jnp.logical_and(on_diagonal, slot == part)
            away = pltpu.make_async_remote_copy(
                src_ref=flat_ref.at[part],
                dst_ref=out_ref.at[slot],
                send_sem=send_sem.at[part],
                recv_sem=recv_sem.at[slot],
                device_id={"row": peer_row, "col": row * parts + part},
                device_id_type=MESH,
            )
            stay = pltpu.make_async_copy(flat_ref.at[part], out_ref.at[part], local_sem)
            pl.when(jnp.logical_not(same))(away.start)
            pl.when(same)(stay.start)
        for part in range(parts):
            same = jnp.logical_and(on_diagonal, slot == part)
            away = pltpu.make_async_remote_copy(
                src_ref=flat_ref.at[part],
                dst_ref=out_ref.at[part],
                send_sem=send_sem.at[part],
                recv_sem=recv_sem.at[part],
                device_id={"row": peer_row, "col": row * parts + part},
                device_id_type=MESH,
            )
            stay = pltpu.make_async_copy(flat_ref.at[part], out_ref.at[part], local_sem)
            pl.when(jnp.logical_not(same))(away.wait)
            pl.when(same)(stay.wait)
        for part in range(parts):
            wide_ref[...] = out_ref[part].astype(jnp.float32)

            @pl.loop(0, tile_cols, unroll=4)
            def _(i, part=part):
                packed = wide_ref[pl.ds(i, half, stride=tile_cols), :]
                other = pltpu.roll(packed, packed.shape[1] - bin_count, axis=1)
                flipped = jnp.concatenate([packed, other], axis=0)
                at = pl.multiple_of((part * tile_cols + i) * tile_cols, 16)
                own = logit_ref[pl.ds(at, tile_cols), :].astype(jnp.float32)
                final = ((own + flipped) * 0.5).astype(jnp.bfloat16)
                final_ref[part * tile_cols + i] = final[:, :bin_count]

    width = flat.shape[2]
    return pl.pallas_call(
        kernel,
        out_shape=jax.ShapeDtypeStruct((tile_rows, tile_cols, bin_count), jnp.bfloat16),
        in_specs=[full_spec()] * 2,
        out_specs=full_spec(),
        scratch_shapes=[
            pltpu.VMEM(flat.shape, flat.dtype),
            pltpu.VMEM((half * tile_cols, width), jnp.float32),
            pltpu.SemaphoreType.DMA((parts,)),
            pltpu.SemaphoreType.DMA((parts,)),
            pltpu.SemaphoreType.DMA,
        ],
        compiler_params=pltpu.CompilerParams(collective_id=own_id, has_side_effects=True),
    )(flat, logit_flat)


def per_device(
    pair_state,
    seq_state,
    residue_index,
    residue_mask,
    position_table,
    attention_gain,
    bias_norm_gain,
    query_weight,
    key_weight,
    value_weight,
    gate_weight,
    out_weight,
    bias_weight,
    outer_gain,
    outer_weight,
    outer_out_weight,
    transition_gain,
    up_weight,
    down_weight,
    distance_weight,
):
    col_total = lax.axis_size("col")
    tile_rows, tile_cols, channels = pair_state.shape
    length = tile_cols * col_total
    row_first = lax.axis_index("row") * tile_rows
    col_first = lax.axis_index("col") * tile_cols
    row_pos = lax.dynamic_slice_in_dim(residue_index, row_first, tile_rows)
    col_pos = lax.dynamic_slice_in_dim(residue_index, col_first, tile_cols)
    row_live = lax.dynamic_slice_in_dim(residue_mask, row_first, tile_rows) > 0
    col_live = lax.dynamic_slice_in_dim(residue_mask, col_first, tile_cols) > 0
    offset = jnp.clip(col_pos[None, :] - row_pos[:, None], -RELPOS_MAX, RELPOS_MAX) + RELPOS_MAX + 1
    bin_index = jnp.where(row_live[:, None] & col_live[None, :], offset, 0)
    table_rows = position_table.shape[0]
    padded_rows = (table_rows + 127) // 128 * 128
    table_padded = jnp.pad(position_table, ((0, padded_rows - table_rows), (0, 0)))
    one_hot = (
        bin_index.reshape(-1, 1) == jnp.arange(padded_rows, dtype=jnp.int32)[None, :]
    ).astype(jnp.bfloat16)
    pair_now = pair_state.astype(jnp.float32) + jnp.dot(
        one_hot, table_padded, preferred_element_type=jnp.float32
    ).reshape(tile_rows, tile_cols, channels)
    pair_flat = pair_now.reshape(-1, channels)
    bias_weight_t = jnp.swapaxes(bias_weight, 1, 2)
    live_column = residue_mask.reshape(-1, 1)
    bin_count = distance_weight.shape[1]
    bins_pair = jnp.stack(
        [
            jnp.pad(distance_weight, ((0, 0), (0, bin_count))),
            jnp.pad(distance_weight, ((0, 0), (bin_count, 0))),
        ]
    )
    layers = query_weight.shape[0]
    extra = bias_step(0, pair_flat, tile_rows, tile_cols, bias_norm_gain, bias_weight_t)
    seq_now, seq_all = seq_state, None
    for layer in range(layers):
        seq_now, seq_all, proj_all = sequence_step(
            layer,
            seq_now,
            seq_all,
            extra,
            live_column,
            (attention_gain, outer_gain),
            (query_weight, key_weight, value_weight, gate_weight, out_weight),
            outer_weight,
            layer,
        )
        pair_flat, extra = pair_step(
            layer,
            layer == layers - 1,
            pair_flat,
            proj_all.reshape(-1, proj_all.shape[2]),
            tile_rows,
            tile_cols,
            (outer_out_weight, up_weight, down_weight),
            (transition_gain, bias_norm_gain),
            bias_weight_t,
            bins_pair,
        )
    distogram = mirror(pair_flat, extra, tile_rows, tile_cols, bin_count, layers)
    return (distogram, seq_now)


def solution(mesh):
    in_specs = (
        P("row", "col", None),
        P("row", "col"),
        P(),
        P(),
        P(),
        P(),
        P(),
        P(None, None, "col"),
        P(None, None, "col"),
        P(None, None, "col"),
        P(None, None, "col"),
        P(None, None, "col"),
        P(),
        P(),
        P(),
        P(),
        P(),
        P(),
        P(),
        P(),
    )
    out_specs = (P("row", "col", None), P("row", "col"))
    return jax.shard_map(
        per_device, mesh=mesh, in_specs=in_specs, out_specs=out_specs, check_vma=False
    )
```

```python
import jax
import jax.numpy as jnp
from jax import lax
from jax.experimental import pallas as pl
from jax.experimental.pallas import tpu as pltpu
from jax.sharding import PartitionSpec as P

HEAD_DIM = 32
RELPOS_MAX = 32
MESH = pl.DeviceIdType.MESH


def normalize(values, weight_gain):
    average = jnp.mean(values, axis=-1, keepdims=True)
    centred = values - average
    spread = jnp.mean(centred * centred, axis=-1, keepdims=True)
    return centred * lax.rsqrt(spread + 1e-05) * weight_gain


def full_spec():
    return pl.BlockSpec(memory_space=pltpu.VMEM)


def lane_join(stacked_ref):
    return jnp.concatenate([stacked_ref[k] for k in range(stacked_ref.shape[0])], axis=1)


def spread(source, target, axis, send_sem, recv_sem):
    total, me = lax.axis_size(axis), lax.axis_index(axis)
    copies = []
    for step in range(1, total):
        peer = lax.rem(me + step, total)
        copies.append(
            pltpu.make_async_remote_copy(
                src_ref=source(peer),
                dst_ref=target(me),
                send_sem=send_sem.at[step - 1],
                recv_sem=recv_sem.at[step - 1],
                device_id={axis: peer},
                device_id_type=MESH,
            )
        )
    for copy in copies:
        copy.start()
    return copies


def finish(copies):
    for copy in copies:
        copy.wait()


def sequence_step(
    layer, seq_tile, seq_all, bias_send, live_column, gains, weights, outer_weight, own_id
):
    nr, nc = lax.axis_size("row"), lax.axis_size("col")
    tr, width = seq_tile.shape
    heads, tc, lanes = bias_send.shape
    hl = heads // nc
    length = nr * tr
    cs = outer_weight.shape[1]
    wide = outer_weight.shape[2]
    first = seq_all is None
    score_scale = HEAD_DIM ** (-0.5)

    def kernel(*refs):
        it = iter(refs)
        seq_ref = next(it)
        seq_all_ref = None if first else next(it)
        bias_ref, live_ref, gain_ref, outer_gain_ref = (next(it) for _ in range(4))
        weight_hbm = [next(it) for _ in range(6)]
        seq_out, seq_out_all, proj_all = (next(it) for _ in range(3))
        weight_refs = [next(it) for _ in range(6)]
        gathered, kv_all, bias_all, gated_all = (next(it) for _ in range(4))
        weight_sem = next(it)
        col_send, col_recv, row_send, row_recv = (next(it) for _ in range(4))

        loads = [
            pltpu.make_async_copy(weight_hbm[k].at[layer], weight_refs[k], weight_sem.at[k])
            for k in range(6)
        ]
        for load in loads:
            load.start()
        row, col = lax.axis_index("row"), lax.axis_index("col")
        barrier = pltpu.get_barrier_semaphore()
        for axis, total, me in (("col", nc, col), ("row", nr, row)):
            for step in range(1, total):
                pl.semaphore_signal(
                    barrier,
                    inc=1,
                    device_id={axis: lax.rem(me + step, total)},
                    device_id_type=MESH,
                )
        pl.semaphore_wait(barrier, nc + nr - 2)
        if first:
            seq_copies = spread(
                lambda peer: seq_ref,
                lambda me: gathered.at[me],
                "col",
                col_send.at[0],
                col_recv.at[0],
            )
        bias_copies = spread(
            lambda peer: bias_ref.at[pl.ds(peer * hl, hl)],
            lambda me: bias_all.at[me],
            "col",
            col_send.at[1],
            col_recv.at[1],
        )
        bias_all[col] = bias_ref[pl.ds(col * hl, hl)]
        if first:
            gathered[col] = seq_ref[...]
            finish(seq_copies)
            entering = lane_join(gathered)
        else:
            entering = lane_join(seq_all_ref)
        normed = normalize(entering.astype(jnp.float32), gain_ref[pl.ds(layer, 1), :]).astype(
            jnp.bfloat16
        )

        def product(value, k):
            return jnp.dot(value, weight_refs[k][...], preferred_element_type=jnp.float32)

        loads[1].wait()
        kv_all[row, 0] = product(normed, 1).astype(jnp.bfloat16)
        loads[2].wait()
        kv_all[row, 1] = product(normed, 2).astype(jnp.bfloat16)
        kv_copies = spread(
            lambda peer: kv_all.at[row],
            lambda me: kv_all.at[me],
            "row",
            row_send.at[0],
            row_recv.at[0],
        )
        loads[0].wait()
        queries = (product(normed, 0) * score_scale).astype(jnp.bfloat16)
        loads[3].wait()
        gating = jax.nn.sigmoid(product(normed, 3))
        head_of = lax.broadcasted_iota(jnp.int32, (tr, width), 1) // HEAD_DIM
        finish(kv_copies)
        finish(bias_copies)
        keys = kv_all[:, 0].reshape(length, width)
        values = kv_all[:, 1].reshape(length, width)
        live = live_ref[...] > 0
        attended = jnp.zeros((tr, width), jnp.float32)
        for head in range(hl):
            own = head_of == head
            query = jnp.where(own, queries.astype(jnp.float32), 0.0).astype(jnp.bfloat16)
            scores = lax.dot_general(
                keys, query, (((1,), (1,)), ((), ())), preferred_element_type=jnp.float32
            )
            bias = bias_all[:, head].reshape(length, lanes)[:, :tr]
            scores = jnp.where(live, scores + bias.astype(jnp.float32), -jnp.inf)
            shifted = jnp.exp(scores - jnp.max(scores, axis=0, keepdims=True))
            share = (shifted / jnp.sum(shifted, axis=0, keepdims=True)).astype(jnp.bfloat16)
            mixed = lax.dot_general(
                share, values, (((0,), (0,)), ((), ())), preferred_element_type=jnp.float32
            )
            attended = jnp.where(own, mixed, attended)
        gated_all[col] = (gating * attended).astype(jnp.bfloat16)
        finish(
            spread(
                lambda peer: gated_all.at[col],
                lambda me: gated_all.at[me],
                "col",
                col_send.at[2],
                col_recv.at[2],
            )
        )
        loads[4].wait()
        leaving = (seq_ref[...].astype(jnp.float32) + product(lane_join(gated_all), 4)).astype(
            jnp.bfloat16
        )
        seq_out_all[col] = leaving
        seq_out[...] = leaving
        finish(
            spread(
                lambda peer: seq_out_all.at[col],
                lambda me: seq_out_all.at[me],
                "col",
                col_send.at[3],
                col_recv.at[3],
            )
        )
        outer_in = normalize(
            lane_join(seq_out_all).astype(jnp.float32), outer_gain_ref[pl.ds(layer, 1), :]
        ).astype(jnp.bfloat16)
        loads[5].wait()
        proj_all[row] = product(outer_in, 5).astype(jnp.bfloat16)
        finish(
            spread(
                lambda peer: proj_all.at[row],
                lambda me: proj_all.at[me],
                "row",
                row_send.at[1],
                row_recv.at[1],
            )
        )

    operands = [seq_tile] + ([] if first else [seq_all]) + [bias_send, live_column, *gains]
    specs = [full_spec()] * len(operands) + [pl.BlockSpec(memory_space=pl.ANY)] * 6
    bf16 = jnp.bfloat16
    return pl.pallas_call(
        kernel,
        out_shape=(
            jax.ShapeDtypeStruct((tr, width), bf16),
            jax.ShapeDtypeStruct((nc, tr, width), bf16),
            jax.ShapeDtypeStruct((nr, tr, wide), bf16),
        ),
        in_specs=specs,
        out_specs=(full_spec(),) * 3,
        scratch_shapes=[pltpu.VMEM((cs, width), bf16)] * 5
        + [
            pltpu.VMEM((cs, wide), bf16),
            pltpu.VMEM((nc, tr, width), bf16),
            pltpu.VMEM((nr, 2, tr, width), bf16),
            pltpu.VMEM((nc, hl, tc, lanes), bf16),
            pltpu.VMEM((nc, tr, width), bf16),
            pltpu.SemaphoreType.DMA((6,)),
            pltpu.SemaphoreType.DMA((4, nc - 1)),
            pltpu.SemaphoreType.DMA((4, nc - 1)),
            pltpu.SemaphoreType.DMA((2, nr - 1)),
            pltpu.SemaphoreType.DMA((2, nr - 1)),
        ],
        compiler_params=pltpu.CompilerParams(collective_id=own_id, has_side_effects=True),
    )(*operands, *weights, outer_weight)


def bias_rows(pair_ref, gain, weight, mixed_ref, out_ref, tr, tc):
    heads = weight.shape[0]

    @pl.loop(0, tc, unroll=12)
    def _(j):
        normed = normalize(pair_ref[pl.ds(j, tr, stride=tc), :], gain).astype(jnp.bfloat16)
        mixed_ref[pl.ds(j * heads, heads), 0:tr] = lax.dot_general(
            weight, normed, (((1,), (1,)), ((), ())), preferred_element_type=jnp.float32
        )

    for head in range(heads):
        out_ref[head] = mixed_ref[pl.ds(head, tc, stride=heads), :].astype(jnp.bfloat16)


def bias_step(layer, pair_flat, tr, tc, bias_norm_gain, bias_weight_t):
    heads = bias_weight_t.shape[1]
    lanes = (tr + 127) // 128 * 128

    def kernel(pair_ref, gain_ref, weight_ref, out_ref, mixed_ref):
        bias_rows(pair_ref, gain_ref[pl.ds(layer, 1), :], weight_ref[layer], mixed_ref, out_ref, tr, tc)

    return pl.pallas_call(
        kernel,
        out_shape=jax.ShapeDtypeStruct((heads, tc, lanes), jnp.bfloat16),
        in_specs=[full_spec()] * 3,
        out_specs=full_spec(),
        scratch_shapes=[pltpu.VMEM((tc * heads, lanes), jnp.float32)],
    )(pair_flat, bias_norm_gain, bias_weight_t)


def pair_step(layer, last, pair_flat, proj_all, tr, tc, mats, gains, bias_weight_t, heads_of_bins):
    channels = pair_flat.shape[1]
    heads = bias_weight_t.shape[1]
    lanes = (tr + 127) // 128 * 128
    rows = 8
    parts = tr // tc
    half = tc // 2

    def kernel(
        pair_ref,
        proj_ref,
        outer_ref,
        up_ref,
        down_ref,
        transition_ref,
        bias_gain_ref,
        bias_weight_ref,
        bins_ref,
        out_ref,
        extra_ref,
        fresh_ref,
        mixed_ref,
        left_ref,
    ):
        row, col = lax.axis_index("row"), lax.axis_index("col")
        low = lax.broadcasted_iota(jnp.int32, (1, channels), 1) < channels // 2
        left = proj_ref[pl.ds(pl.multiple_of(row * tr, 16), tr), :].astype(jnp.float32)
        left_ref[...] = jnp.where(low, left, pltpu.roll(left, channels // 2, axis=1))
        right = proj_ref[pl.ds(pl.multiple_of(col * tc, 16), tc), :].astype(jnp.float32)
        right = jnp.where(low, pltpu.roll(right, channels // 2, axis=1), right)[None]
        gain = transition_ref[pl.ds(layer, 1), :]

        @pl.loop(0, tr // rows, unroll=3)
        def _(step):
            at = pl.ds(pl.multiple_of(step * (rows * tc), rows * tc), rows * tc)
            left = left_ref[pl.ds(pl.multiple_of(step * rows, rows), rows), :][:, None, :]
            features = jnp.where(low[None], left * right, left - right)
            features = features.reshape(rows * tc, channels).astype(jnp.bfloat16)
            middle = pair_ref[at, :].astype(jnp.float32) + jnp.dot(
                features, outer_ref[layer], preferred_element_type=jnp.float32
            )
            normed = normalize(middle, gain).astype(jnp.bfloat16)
            hidden = jnp.maximum(
                jnp.dot(normed, up_ref[layer], preferred_element_type=jnp.float32), 0.0
            ).astype(jnp.bfloat16)
            fresh = (
                middle + jnp.dot(hidden, down_ref[layer], preferred_element_type=jnp.float32)
            ).astype(jnp.bfloat16)
            if last:
                fresh_ref[at, :] = fresh.astype(jnp.float32)
                out_ref[at, :] = jnp.dot(
                    fresh, bins_ref[0], preferred_element_type=jnp.float32
                ).astype(jnp.bfloat16)
            else:
                out_ref[at, :] = fresh
                fresh_ref[at, :] = fresh.astype(jnp.float32)

        if last:
            count = half * tc
            for part in range(parts):
                near = fresh_ref[pl.ds(part * 2 * count, count), :].astype(jnp.bfloat16)
                far = fresh_ref[pl.ds((part * 2 + 1) * count, count), :].astype(jnp.bfloat16)
                extra_ref[part] = (
                    jnp.dot(near, bins_ref[0], preferred_element_type=jnp.float32)
                    + jnp.dot(far, bins_ref[1], preferred_element_type=jnp.float32)
                ).astype(jnp.bfloat16)
        else:
            bias_rows(
                fresh_ref,
                bias_gain_ref[pl.ds(layer + 1, 1), :],
                bias_weight_ref[layer + 1],
                mixed_ref,
                extra_ref,
                tr,
                tc,
            )

    width = heads_of_bins.shape[2]
    extra = (parts, half * tc, width) if last else (heads, tc, lanes)
    operands = (pair_flat, proj_all, *mats, *gains, bias_weight_t, heads_of_bins)
    return pl.pallas_call(
        kernel,
        out_shape=(
            jax.ShapeDtypeStruct((tr * tc, width if last else channels), jnp.bfloat16),
            jax.ShapeDtypeStruct(extra, jnp.bfloat16),
        ),
        in_specs=[full_spec()] * len(operands),
        out_specs=(full_spec(),) * 2,
        scratch_shapes=[
            pltpu.VMEM((tr * tc, channels), jnp.float32),
            pltpu.VMEM((tc * heads, lanes), jnp.float32),
            pltpu.VMEM((tr, channels), jnp.float32),
        ],
    )(*operands)


def mirror(logit_flat, flat, tile_rows, tile_cols, bin_count, own_id):
    nr, nc = lax.axis_size("row"), lax.axis_size("col")
    parts = tile_rows // tile_cols
    half = tile_cols // 2
    width = flat.shape[2]
    depth = flat.shape[1] // nc
    flat = flat.reshape(parts, nc, depth, width)

    def kernel(
        flat_ref,
        logit_ref,
        final_ref,
        spread_ref,
        moved_ref,
        landed_ref,
        wide_ref,
        send_1,
        send_2,
        send_3,
        recv_1,
        recv_2,
        recv_3,
    ):
        row, col = lax.axis_index("row"), lax.axis_index("col")
        barrier = pltpu.get_barrier_semaphore()
        for axis, total, me in (("col", nc, col), ("row", nr, row)):
            for step in range(1, total):
                pl.semaphore_signal(
                    barrier,
                    inc=1,
                    device_id={axis: lax.rem(me + step, total)},
                    device_id_type=MESH,
                )
        pl.semaphore_wait(barrier, nc + nr - 2)

        def away(source, target, send, recv, axis, peer):
            return pltpu.make_async_remote_copy(
                src_ref=source,
                dst_ref=target,
                send_sem=send,
                recv_sem=recv,
                device_id={axis: peer},
                device_id_type=MESH,
            )

        sent = []

        def forward(source, target, send, recv, axis, peer, me):
            remote = away(source, target, send, recv, axis, peer)
            stay = pltpu.make_async_copy(source, target, recv)
            same = peer == me
            pl.when(jnp.logical_not(same))(remote.start)
            pl.when(same)(stay.start)
            sent.append((same, remote))

        def arrive(target, recv):
            pltpu.make_async_copy(target, target, recv).wait()

        for step in range(nc):
            peer = lax.rem(col + step, nc)
            for part in range(parts):
                if step:
                    remote = away(
                        flat_ref.at[part, peer],
                        spread_ref.at[col, part],
                        send_1.at[step, part],
                        recv_1.at[col, part],
                        "col",
                        peer,
                    )
                    remote.start()
                    sent.append((None, remote))
        for step in range(nc):
            origin = lax.rem(col + nc - step, nc)
            peer, slot = lax.div(origin, parts), lax.rem(origin, parts)
            for part in range(parts):
                if step:
                    arrive(spread_ref.at[origin, part], recv_1.at[origin, part])
                forward(
                    spread_ref.at[origin, part] if step else flat_ref.at[part, col],
                    moved_ref.at[row, slot, part],
                    send_2.at[step, part],
                    recv_2.at[row, slot, part],
                    "row",
                    peer,
                    row,
                )
        for step in range(nr):
            origin = lax.rem(row + step, nr)
            for slot in range(parts):
                for part in range(parts):
                    arrive(moved_ref.at[origin, slot, part], recv_2.at[origin, slot, part])
                    forward(
                        moved_ref.at[origin, slot, part],
                        landed_ref.at[col, slot],
                        send_3.at[step, slot, part],
                        recv_3.at[col, slot],
                        "col",
                        origin * parts + part,
                        col,
                    )
        for slot in range(parts):
            for piece in range(nc):
                arrive(landed_ref.at[piece, slot], recv_3.at[piece, slot])
                wide_ref[piece * depth : (piece + 1) * depth, :] = landed_ref[
                    piece, slot
                ].astype(jnp.float32)

            @pl.loop(0, tile_cols, unroll=8)
            def _(i, slot=slot):
                packed = wide_ref[pl.ds(i, half, stride=tile_cols), :]
                other = pltpu.roll(packed, width - bin_count, axis=1)
                flipped = jnp.concatenate([packed, other], axis=0)
                at = pl.multiple_of((slot * tile_cols + i) * tile_cols, 16)
                own = logit_ref[pl.ds(at, tile_cols), :].astype(jnp.float32)
                final = ((own + flipped) * 0.5).astype(jnp.bfloat16)
                final_ref[slot * tile_cols + i] = final[:, :bin_count]

        for same, remote in sent:
            if same is None:
                remote.wait_send()
            else:
                pl.when(jnp.logical_not(same))(remote.wait_send)

    dma = pltpu.SemaphoreType.DMA
    return pl.pallas_call(
        kernel,
        out_shape=jax.ShapeDtypeStruct((tile_rows, tile_cols, bin_count), jnp.bfloat16),
        in_specs=[full_spec()] * 2,
        out_specs=full_spec(),
        scratch_shapes=[
            pltpu.VMEM((nc, parts, depth, width), flat.dtype),
            pltpu.VMEM((nr, parts, parts, depth, width), flat.dtype),
            pltpu.VMEM((nc, parts, depth, width), flat.dtype),
            pltpu.VMEM((nc * depth, width), jnp.float32),
            dma((nc, parts)),
            dma((nc, parts)),
            dma((nr, parts, parts)),
            dma((nc, parts)),
            dma((nr, parts, parts)),
            dma((nc, parts)),
        ],
        compiler_params=pltpu.CompilerParams(collective_id=own_id, has_side_effects=True),
    )(flat, logit_flat)


def per_device(
    pair_state,
    seq_state,
    residue_index,
    residue_mask,
    position_table,
    attention_gain,
    bias_norm_gain,
    query_weight,
    key_weight,
    value_weight,
    gate_weight,
    out_weight,
    bias_weight,
    outer_gain,
    outer_weight,
    outer_out_weight,
    transition_gain,
    up_weight,
    down_weight,
    distance_weight,
):
    col_total = lax.axis_size("col")
    tile_rows, tile_cols, channels = pair_state.shape
    length = tile_cols * col_total
    row_first = lax.axis_index("row") * tile_rows
    col_first = lax.axis_index("col") * tile_cols
    row_pos = lax.dynamic_slice_in_dim(residue_index, row_first, tile_rows)
    col_pos = lax.dynamic_slice_in_dim(residue_index, col_first, tile_cols)
    row_live = lax.dynamic_slice_in_dim(residue_mask, row_first, tile_rows) > 0
    col_live = lax.dynamic_slice_in_dim(residue_mask, col_first, tile_cols) > 0
    offset = jnp.clip(col_pos[None, :] - row_pos[:, None], -RELPOS_MAX, RELPOS_MAX) + RELPOS_MAX + 1
    bin_index = jnp.where(row_live[:, None] & col_live[None, :], offset, 0)
    table_rows = position_table.shape[0]
    padded_rows = (table_rows + 127) // 128 * 128
    table_padded = jnp.pad(position_table, ((0, padded_rows - table_rows), (0, 0)))
    one_hot = (
        bin_index.reshape(-1, 1) == jnp.arange(padded_rows, dtype=jnp.int32)[None, :]
    ).astype(jnp.bfloat16)
    pair_now = pair_state.astype(jnp.float32) + jnp.dot(
        one_hot, table_padded, preferred_element_type=jnp.float32
    ).reshape(tile_rows, tile_cols, channels)
    pair_flat = pair_now.reshape(-1, channels)
    bias_weight_t = jnp.swapaxes(bias_weight, 1, 2)
    live_column = residue_mask.reshape(-1, 1)
    bin_count = distance_weight.shape[1]
    bins_pair = jnp.stack(
        [
            jnp.pad(distance_weight, ((0, 0), (0, bin_count))),
            jnp.pad(distance_weight, ((0, 0), (bin_count, 0))),
        ]
    )
    layers = query_weight.shape[0]
    extra = bias_step(0, pair_flat, tile_rows, tile_cols, bias_norm_gain, bias_weight_t)
    seq_now, seq_all = seq_state, None
    for layer in range(layers):
        seq_now, seq_all, proj_all = sequence_step(
            layer,
            seq_now,
            seq_all,
            extra,
            live_column,
            (attention_gain, outer_gain),
            (query_weight, key_weight, value_weight, gate_weight, out_weight),
            outer_weight,
            layer,
        )
        pair_flat, extra = pair_step(
            layer,
            layer == layers - 1,
            pair_flat,
            proj_all.reshape(-1, proj_all.shape[2]),
            tile_rows,
            tile_cols,
            (outer_out_weight, up_weight, down_weight),
            (transition_gain, bias_norm_gain),
            bias_weight_t,
            bins_pair,
        )
    distogram = mirror(pair_flat, extra, tile_rows, tile_cols, bin_count, layers)
    return (distogram, seq_now)


def solution(mesh):
    in_specs = (
        P("row", "col", None),
        P("row", "col"),
        P(),
        P(),
        P(),
        P(),
        P(),
        P(None, None, "col"),
        P(None, None, "col"),
        P(None, None, "col"),
        P(None, None, "col"),
        P(None, None, "col"),
        P(),
        P(),
        P(),
        P(),
        P(),
        P(),
        P(),
        P(),
    )
    out_specs = (P("row", "col", None), P("row", "col"))
    return jax.shard_map(
        per_device, mesh=mesh, in_specs=in_specs, out_specs=out_specs, check_vma=False
    )
```

```python
import jax
import jax.numpy as jnp
from jax import lax
from jax.experimental import pallas as pl
from jax.experimental.pallas import tpu as pltpu
from jax.sharding import PartitionSpec as P

HEAD_DIM = 32
RELPOS_MAX = 32
MESH = pl.DeviceIdType.MESH


def normalize(values, weight_gain):
    average = jnp.mean(values, axis=-1, keepdims=True)
    centred = values - average
    spread = jnp.mean(centred * centred, axis=-1, keepdims=True)
    return centred * lax.rsqrt(spread + 1e-05) * weight_gain


def full_spec():
    return pl.BlockSpec(memory_space=pltpu.VMEM)


def lane_join(stacked_ref):
    return jnp.concatenate([stacked_ref[k] for k in range(stacked_ref.shape[0])], axis=1)


def spread(source, target, axis, send_sem, recv_sem):
    total, me = lax.axis_size(axis), lax.axis_index(axis)
    copies = []
    for step in range(1, total):
        peer = lax.rem(me + step, total)
        copies.append(
            pltpu.make_async_remote_copy(
                src_ref=source(peer),
                dst_ref=target(me),
                send_sem=send_sem.at[step - 1],
                recv_sem=recv_sem.at[step - 1],
                device_id={axis: peer},
                device_id_type=MESH,
            )
        )
    for copy in copies:
        copy.start()
    return copies


def finish(copies):
    for copy in copies:
        copy.wait()


def sequence_step(
    layer, seq_tile, seq_all, bias_send, live_column, gains, weights, outer_weight, own_id
):
    nr, nc = lax.axis_size("row"), lax.axis_size("col")
    tr, width = seq_tile.shape
    heads, tc, lanes = bias_send.shape
    hl = heads // nc
    length = nr * tr
    cs = outer_weight.shape[1]
    wide = outer_weight.shape[2]
    first = seq_all is None
    score_scale = HEAD_DIM ** (-0.5)

    def kernel(*refs):
        it = iter(refs)
        seq_ref = next(it)
        seq_all_ref = None if first else next(it)
        bias_ref, live_ref, gain_ref, outer_gain_ref = (next(it) for _ in range(4))
        weight_hbm = [next(it) for _ in range(6)]
        seq_out, seq_out_all, left_out, right_out = (next(it) for _ in range(4))
        weight_refs = [next(it) for _ in range(6)]
        gathered, kv_all, bias_all, gated_all, right_send = (next(it) for _ in range(5))
        weight_sem = next(it)
        col_send, col_recv, row_send, row_recv = (next(it) for _ in range(4))

        loads = [
            pltpu.make_async_copy(weight_hbm[k].at[layer], weight_refs[k], weight_sem.at[k])
            for k in range(6)
        ]
        for load in loads:
            load.start()
        row, col = lax.axis_index("row"), lax.axis_index("col")
        barrier = pltpu.get_barrier_semaphore()
        for axis, total, me in (("col", nc, col), ("row", nr, row)):
            for step in range(1, total):
                pl.semaphore_signal(
                    barrier,
                    inc=1,
                    device_id={axis: lax.rem(me + step, total)},
                    device_id_type=MESH,
                )
        pl.semaphore_wait(barrier, nc + nr - 2)
        if first:
            seq_copies = spread(
                lambda peer: seq_ref,
                lambda me: gathered.at[me],
                "col",
                col_send.at[0],
                col_recv.at[0],
            )
        bias_copies = spread(
            lambda peer: bias_ref.at[pl.ds(peer * hl, hl)],
            lambda me: bias_all.at[me],
            "col",
            col_send.at[1],
            col_recv.at[1],
        )
        bias_all[col] = bias_ref[pl.ds(col * hl, hl)]
        if first:
            gathered[col] = seq_ref[...]
            finish(seq_copies)
            entering = lane_join(gathered)
        else:
            entering = lane_join(seq_all_ref)
        normed = normalize(entering.astype(jnp.float32), gain_ref[pl.ds(layer, 1), :]).astype(
            jnp.bfloat16
        )

        def product(value, k):
            return jnp.dot(value, weight_refs[k][...], preferred_element_type=jnp.float32)

        loads[1].wait()
        kv_all[row, 0] = product(normed, 1).astype(jnp.bfloat16)
        loads[2].wait()
        kv_all[row, 1] = product(normed, 2).astype(jnp.bfloat16)
        kv_copies = spread(
            lambda peer: kv_all.at[row],
            lambda me: kv_all.at[me],
            "row",
            row_send.at[0],
            row_recv.at[0],
        )
        loads[0].wait()
        queries = (product(normed, 0) * score_scale).astype(jnp.bfloat16)
        loads[3].wait()
        gating = jax.nn.sigmoid(product(normed, 3))
        head_of = lax.broadcasted_iota(jnp.int32, (tr, width), 1) // HEAD_DIM
        finish(kv_copies)
        finish(bias_copies)
        keys = kv_all[:, 0].reshape(length, width)
        values = kv_all[:, 1].reshape(length, width)
        live = live_ref[...] > 0
        attended = jnp.zeros((tr, width), jnp.float32)
        for head in range(hl):
            own = head_of == head
            query = jnp.where(own, queries.astype(jnp.float32), 0.0).astype(jnp.bfloat16)
            scores = lax.dot_general(
                keys, query, (((1,), (1,)), ((), ())), preferred_element_type=jnp.float32
            )
            bias = bias_all[:, head].reshape(length, lanes)[:, :tr]
            scores = jnp.where(live, scores + bias.astype(jnp.float32), -jnp.inf)
            shifted = jnp.exp(scores - jnp.max(scores, axis=0, keepdims=True))
            share = (shifted / jnp.sum(shifted, axis=0, keepdims=True)).astype(jnp.bfloat16)
            mixed = lax.dot_general(
                share, values, (((0,), (0,)), ((), ())), preferred_element_type=jnp.float32
            )
            attended = jnp.where(own, mixed, attended)
        gated_all[col] = (gating * attended).astype(jnp.bfloat16)
        finish(
            spread(
                lambda peer: gated_all.at[col],
                lambda me: gated_all.at[me],
                "col",
                col_send.at[2],
                col_recv.at[2],
            )
        )
        loads[4].wait()
        leaving = (seq_ref[...].astype(jnp.float32) + product(lane_join(gated_all), 4)).astype(
            jnp.bfloat16
        )
        seq_out_all[col] = leaving
        seq_out[...] = leaving
        finish(
            spread(
                lambda peer: seq_out_all.at[col],
                lambda me: seq_out_all.at[me],
                "col",
                col_send.at[3],
                col_recv.at[3],
            )
        )
        outer_in = normalize(
            lane_join(seq_out_all).astype(jnp.float32), outer_gain_ref[pl.ds(layer, 1), :]
        ).astype(jnp.bfloat16)
        loads[5].wait()
        projected = product(outer_in, 5)
        left_out[...] = projected.astype(jnp.bfloat16)
        parts = tr // tc
        holder = lax.div(col, parts)
        right_send[...] = left_out[pl.ds(pl.multiple_of(lax.rem(col, parts) * tc, 16), tc), :]
        right_copies = [
            pltpu.make_async_remote_copy(
                src_ref=right_send,
                dst_ref=right_out,
                send_sem=row_send.at[1, step - 1],
                recv_sem=row_recv.at[1, 0],
                device_id={"row": lax.rem(row + step, nr)},
                device_id_type=MESH,
            )
            for step in range(1, nr)
        ]

        @pl.when(row == holder)
        def _():
            for copy in right_copies:
                copy.start()
            right_out[...] = right_send[...]
            for copy in right_copies:
                copy.wait_send()

        pl.when(row != holder)(right_copies[0].wait_recv)

    operands = [seq_tile] + ([] if first else [seq_all]) + [bias_send, live_column, *gains]
    specs = [full_spec()] * len(operands) + [pl.BlockSpec(memory_space=pl.ANY)] * 6
    bf16 = jnp.bfloat16
    return pl.pallas_call(
        kernel,
        out_shape=(
            jax.ShapeDtypeStruct((tr, width), bf16),
            jax.ShapeDtypeStruct((nc, tr, width), bf16),
            jax.ShapeDtypeStruct((tr, wide), bf16),
            jax.ShapeDtypeStruct((tc, wide), bf16),
        ),
        in_specs=specs,
        out_specs=(full_spec(),) * 4,
        scratch_shapes=[pltpu.VMEM((cs, width), bf16)] * 5
        + [
            pltpu.VMEM((cs, wide), bf16),
            pltpu.VMEM((nc, tr, width), bf16),
            pltpu.VMEM((nr, 2, tr, width), bf16),
            pltpu.VMEM((nc, hl, tc, lanes), bf16),
            pltpu.VMEM((nc, tr, width), bf16),
            pltpu.VMEM((tc, wide), bf16),
            pltpu.SemaphoreType.DMA((6,)),
            pltpu.SemaphoreType.DMA((4, nc - 1)),
            pltpu.SemaphoreType.DMA((4, nc - 1)),
            pltpu.SemaphoreType.DMA((2, nr - 1)),
            pltpu.SemaphoreType.DMA((2, nr - 1)),
        ],
        compiler_params=pltpu.CompilerParams(collective_id=own_id, has_side_effects=True),
    )(*operands, *weights, outer_weight)


def bias_rows(pair_ref, gain, weight, mixed_ref, out_ref, tr, tc):
    heads = weight.shape[0]

    @pl.loop(0, tc, unroll=12)
    def _(j):
        normed = normalize(pair_ref[pl.ds(j, tr, stride=tc), :], gain).astype(jnp.bfloat16)
        mixed_ref[pl.ds(j * heads, heads), 0:tr] = lax.dot_general(
            weight, normed, (((1,), (1,)), ((), ())), preferred_element_type=jnp.float32
        )

    for head in range(heads):
        out_ref[head] = mixed_ref[pl.ds(head, tc, stride=heads), :].astype(jnp.bfloat16)


def bias_step(layer, pair_flat, tr, tc, bias_norm_gain, bias_weight_t):
    heads = bias_weight_t.shape[1]
    lanes = (tr + 127) // 128 * 128

    def kernel(pair_ref, gain_ref, weight_ref, out_ref, mixed_ref):
        bias_rows(pair_ref, gain_ref[pl.ds(layer, 1), :], weight_ref[layer], mixed_ref, out_ref, tr, tc)

    return pl.pallas_call(
        kernel,
        out_shape=jax.ShapeDtypeStruct((heads, tc, lanes), jnp.bfloat16),
        in_specs=[full_spec()] * 3,
        out_specs=full_spec(),
        scratch_shapes=[pltpu.VMEM((tc * heads, lanes), jnp.float32)],
    )(pair_flat, bias_norm_gain, bias_weight_t)


def pair_rows(layer, pair_ref, left_ref, right_ref, mats, transition_ref, duplicated_ref, tr, tc):
    channels = pair_ref.shape[1]
    rows = 8
    outer_ref, up_ref, down_ref = mats
    low = lax.broadcasted_iota(jnp.int32, (1, channels), 1) < channels // 2
    left = left_ref[...].astype(jnp.float32)
    duplicated_ref[...] = jnp.where(low, left, pltpu.roll(left, channels // 2, axis=1))
    right = right_ref[...].astype(jnp.float32)
    right = jnp.where(low, pltpu.roll(right, channels // 2, axis=1), right)[None]
    gain = transition_ref[pl.ds(layer, 1), :]

    def update(first, last, store):
        @pl.loop(first // rows, last // rows, unroll=3)
        def _(step):
            at = pl.ds(pl.multiple_of(step * (rows * tc), rows * tc), rows * tc)
            left = duplicated_ref[pl.ds(pl.multiple_of(step * rows, rows), rows), :][:, None, :]
            features = jnp.where(low[None], left * right, left - right)
            features = features.reshape(rows * tc, channels).astype(jnp.bfloat16)
            middle = pair_ref[at, :].astype(jnp.float32) + jnp.dot(
                features, outer_ref[layer], preferred_element_type=jnp.float32
            )
            normed = normalize(middle, gain).astype(jnp.bfloat16)
            hidden = jnp.maximum(
                jnp.dot(normed, up_ref[layer], preferred_element_type=jnp.float32), 0.0
            ).astype(jnp.bfloat16)
            store(
                at,
                (
                    middle + jnp.dot(hidden, down_ref[layer], preferred_element_type=jnp.float32)
                ).astype(jnp.bfloat16),
            )

    return update


def pair_step(layer, pair_flat, left, right, tr, tc, mats, gains, bias_weight_t):
    channels = pair_flat.shape[1]
    heads = bias_weight_t.shape[1]
    lanes = (tr + 127) // 128 * 128

    def kernel(
        pair_ref,
        left_ref,
        right_ref,
        outer_ref,
        up_ref,
        down_ref,
        transition_ref,
        bias_gain_ref,
        bias_weight_ref,
        out_ref,
        bias_ref,
        fresh_ref,
        mixed_ref,
        duplicated_ref,
    ):
        def store(at, fresh):
            out_ref[at, :] = fresh
            fresh_ref[at, :] = fresh.astype(jnp.float32)

        mats_refs = (outer_ref, up_ref, down_ref)
        update = pair_rows(
            layer, pair_ref, left_ref, right_ref, mats_refs, transition_ref, duplicated_ref, tr, tc
        )
        update(0, tr, store)
        bias_rows(
            fresh_ref,
            bias_gain_ref[pl.ds(layer + 1, 1), :],
            bias_weight_ref[layer + 1],
            mixed_ref,
            bias_ref,
            tr,
            tc,
        )

    operands = (pair_flat, left, right, *mats, *gains, bias_weight_t)
    return pl.pallas_call(
        kernel,
        out_shape=(
            jax.ShapeDtypeStruct((tr * tc, channels), jnp.bfloat16),
            jax.ShapeDtypeStruct((heads, tc, lanes), jnp.bfloat16),
        ),
        in_specs=[full_spec()] * len(operands),
        out_specs=(full_spec(),) * 2,
        scratch_shapes=[
            pltpu.VMEM((tr * tc, channels), jnp.float32),
            pltpu.VMEM((tc * heads, lanes), jnp.float32),
            pltpu.VMEM((tr, channels), jnp.float32),
        ],
    )(*operands)


def last_step(layer, pair_flat, left, right, tile_rows, tile_cols, mats, gain, bins_pair, own_id):
    nr, nc = lax.axis_size("row"), lax.axis_size("col")
    parts = tile_rows // tile_cols
    half = tile_cols // 2
    channels = pair_flat.shape[1]
    width = bins_pair.shape[2]
    bin_count = width // 2
    count = half * tile_cols
    depth = count // nc

    def kernel(
        pair_ref,
        left_ref,
        right_ref,
        outer_ref,
        up_ref,
        down_ref,
        gain_ref,
        bins_ref,
        final_ref,
        flat_ref,
        logit_ref,
        fresh_ref,
        duplicated_ref,
        spread_ref,
        moved_ref,
        landed_ref,
        wide_ref,
        send_1,
        send_2,
        send_3,
        recv_1,
        recv_2,
        recv_3,
    ):
        row, col = lax.axis_index("row"), lax.axis_index("col")
        barrier = pltpu.get_barrier_semaphore()
        for axis, total, me in (("col", nc, col), ("row", nr, row)):
            for step in range(1, total):
                pl.semaphore_signal(
                    barrier,
                    inc=1,
                    device_id={axis: lax.rem(me + step, total)},
                    device_id_type=MESH,
                )
        pl.semaphore_wait(barrier, nc + nr - 2)

        def store(at, fresh):
            fresh_ref[at, :] = fresh.astype(jnp.float32)
            logit_ref[at, :] = jnp.dot(
                fresh, bins_ref[0], preferred_element_type=jnp.float32
            ).astype(jnp.bfloat16)

        update = pair_rows(
            layer,
            pair_ref,
            left_ref,
            right_ref,
            (outer_ref, up_ref, down_ref),
            gain_ref,
            duplicated_ref,
            tile_rows,
            tile_cols,
        )

        def away(source, target, send, recv, axis, peer):
            return pltpu.make_async_remote_copy(
                src_ref=source,
                dst_ref=target,
                send_sem=send,
                recv_sem=recv,
                device_id={axis: peer},
                device_id_type=MESH,
            )

        sent = []

        def forward(source, target, send, recv, axis, peer, me):
            remote = away(source, target, send, recv, axis, peer)
            stay = pltpu.make_async_copy(source, target, recv)
            same = peer == me
            pl.when(jnp.logical_not(same))(remote.start)
            pl.when(same)(stay.start)
            sent.append((same, remote))

        def arrive(target, recv):
            pltpu.make_async_copy(target, target, recv).wait()

        for part in range(parts):
            update(part * tile_cols, (part + 1) * tile_cols, store)
            near = fresh_ref[pl.ds(part * 2 * count, count), :].astype(jnp.bfloat16)
            far = fresh_ref[pl.ds((part * 2 + 1) * count, count), :].astype(jnp.bfloat16)
            packed = jnp.dot(near, bins_ref[0], preferred_element_type=jnp.float32) + jnp.dot(
                far, bins_ref[1], preferred_element_type=jnp.float32
            )
            for piece in range(nc):
                flat_ref[part, piece] = packed[piece * depth : (piece + 1) * depth].astype(
                    jnp.bfloat16
                )
            for step in range(1, nc):
                peer = lax.rem(col + step, nc)
                remote = away(
                    flat_ref.at[part, peer],
                    spread_ref.at[col, part],
                    send_1.at[step, part],
                    recv_1.at[col, part],
                    "col",
                    peer,
                )
                remote.start()
                sent.append((None, remote))
        for part in range(parts):
            for step in range(nc):
                origin = lax.rem(col + nc - step, nc)
                peer, slot = lax.div(origin, parts), lax.rem(origin, parts)
                if step:
                    arrive(spread_ref.at[origin, part], recv_1.at[origin, part])
                forward(
                    spread_ref.at[origin, part] if step else flat_ref.at[part, col],
                    moved_ref.at[row, slot, part],
                    send_2.at[step, part],
                    recv_2.at[row, slot, part],
                    "row",
                    peer,
                    row,
                )
        for step in range(nr):
            origin = lax.rem(row + step, nr)
            for slot in range(parts):
                for part in range(parts):
                    arrive(moved_ref.at[origin, slot, part], recv_2.at[origin, slot, part])
                    forward(
                        moved_ref.at[origin, slot, part],
                        landed_ref.at[col, slot],
                        send_3.at[step, slot, part],
                        recv_3.at[col, slot],
                        "col",
                        origin * parts + part,
                        col,
                    )
        for slot in range(parts):
            for piece in range(nc):
                arrive(landed_ref.at[piece, slot], recv_3.at[piece, slot])
                wide_ref[piece * depth : (piece + 1) * depth, :] = landed_ref[
                    piece, slot
                ].astype(jnp.float32)

            @pl.loop(0, tile_cols, unroll=8)
            def _(i, slot=slot):
                packed = wide_ref[pl.ds(i, half, stride=tile_cols), :]
                other = pltpu.roll(packed, width - bin_count, axis=1)
                flipped = jnp.concatenate([packed, other], axis=0)
                at = pl.multiple_of((slot * tile_cols + i) * tile_cols, 16)
                own = logit_ref[pl.ds(at, tile_cols), :].astype(jnp.float32)
                final = ((own + flipped) * 0.5).astype(jnp.bfloat16)
                final_ref[slot * tile_cols + i] = final[:, :bin_count]

        for same, remote in sent:
            if same is None:
                remote.wait_send()
            else:
                pl.when(jnp.logical_not(same))(remote.wait_send)

    operands = (pair_flat, left, right, *mats, gain, bins_pair)
    bf16 = jnp.bfloat16
    dma = pltpu.SemaphoreType.DMA
    return pl.pallas_call(
        kernel,
        out_shape=jax.ShapeDtypeStruct((tile_rows, tile_cols, bin_count), jnp.bfloat16),
        in_specs=[full_spec()] * len(operands),
        out_specs=full_spec(),
        scratch_shapes=[
            pltpu.VMEM((parts, nc, depth, width), bf16),
            pltpu.VMEM((tile_rows * tile_cols, width), bf16),
            pltpu.VMEM((tile_rows * tile_cols, channels), jnp.float32),
            pltpu.VMEM((tile_rows, channels), jnp.float32),
            pltpu.VMEM((nc, parts, depth, width), bf16),
            pltpu.VMEM((nr, parts, parts, depth, width), bf16),
            pltpu.VMEM((nc, parts, depth, width), bf16),
            pltpu.VMEM((nc * depth, width), jnp.float32),
            dma((nc, parts)),
            dma((nc, parts)),
            dma((nr, parts, parts)),
            dma((nc, parts)),
            dma((nr, parts, parts)),
            dma((nc, parts)),
        ],
        compiler_params=pltpu.CompilerParams(collective_id=own_id, has_side_effects=True),
    )(*operands)


def per_device(
    pair_state,
    seq_state,
    residue_index,
    residue_mask,
    position_table,
    attention_gain,
    bias_norm_gain,
    query_weight,
    key_weight,
    value_weight,
    gate_weight,
    out_weight,
    bias_weight,
    outer_gain,
    outer_weight,
    outer_out_weight,
    transition_gain,
    up_weight,
    down_weight,
    distance_weight,
):
    col_total = lax.axis_size("col")
    tile_rows, tile_cols, channels = pair_state.shape
    length = tile_cols * col_total
    row_first = lax.axis_index("row") * tile_rows
    col_first = lax.axis_index("col") * tile_cols
    coded = jnp.where(residue_mask > 0, residue_index, -1)
    row_pos = lax.dynamic_slice_in_dim(coded, row_first, tile_rows)
    col_pos = lax.dynamic_slice_in_dim(coded, col_first, tile_cols)
    offset = jnp.clip(col_pos[None, :] - row_pos[:, None], -RELPOS_MAX, RELPOS_MAX) + RELPOS_MAX + 1
    both_live = (row_pos[:, None] >= 0) & (col_pos[None, :] >= 0)
    bin_index = jnp.where(both_live, offset, 0)
    table_rows = position_table.shape[0]
    padded_rows = (table_rows + 127) // 128 * 128
    table_padded = jnp.pad(position_table, ((0, padded_rows - table_rows), (0, 0)))
    one_hot = (
        bin_index.reshape(-1, 1) == jnp.arange(padded_rows, dtype=jnp.int32)[None, :]
    ).astype(jnp.bfloat16)
    pair_now = pair_state.astype(jnp.float32) + jnp.dot(
        one_hot, table_padded, preferred_element_type=jnp.float32
    ).reshape(tile_rows, tile_cols, channels)
    pair_flat = pair_now.reshape(-1, channels)
    bias_weight_t = jnp.swapaxes(bias_weight, 1, 2)
    live_column = residue_mask.reshape(-1, 1)
    bin_count = distance_weight.shape[1]
    bins_pair = jnp.stack(
        [
            jnp.pad(distance_weight, ((0, 0), (0, bin_count))),
            jnp.pad(distance_weight, ((0, 0), (bin_count, 0))),
        ]
    )
    layers = query_weight.shape[0]
    extra = bias_step(0, pair_flat, tile_rows, tile_cols, bias_norm_gain, bias_weight_t)
    seq_now, seq_all = seq_state, None
    for layer in range(layers):
        seq_now, seq_all, left, right = sequence_step(
            layer,
            seq_now,
            seq_all,
            extra,
            live_column,
            (attention_gain, outer_gain),
            (query_weight, key_weight, value_weight, gate_weight, out_weight),
            outer_weight,
            layer,
        )
        mats = (outer_out_weight, up_weight, down_weight)
        if layer < layers - 1:
            pair_flat, extra = pair_step(
                layer,
                pair_flat,
                left,
                right,
                tile_rows,
                tile_cols,
                mats,
                (transition_gain, bias_norm_gain),
                bias_weight_t,
            )
    distogram = last_step(
        layers - 1,
        pair_flat,
        left,
        right,
        tile_rows,
        tile_cols,
        mats,
        transition_gain,
        bins_pair,
        layers,
    )
    return (distogram, seq_now)


def solution(mesh):
    in_specs = (
        P("row", "col", None),
        P("row", "col"),
        P(),
        P(),
        P(),
        P(),
        P(),
        P(None, None, "col"),
        P(None, None, "col"),
        P(None, None, "col"),
        P(None, None, "col"),
        P(None, None, "col"),
        P(),
        P(),
        P(),
        P(),
        P(),
        P(),
        P(),
        P(),
    )
    out_specs = (P("row", "col", None), P("row", "col"))
    return jax.shard_map(
        per_device, mesh=mesh, in_specs=in_specs, out_specs=out_specs, check_vma=False
    )
```
